256 devices in a mesh: dp: 16 (over z, core), expert: 16 (over y, x).
Axes of the slice: x: 4, y: 4, z: 8, core: 2. Of those that a mesh axis runs over, the one named last changes fastest.
Arguments:
- tokens: bfloat16 [32768, 2048], P(('dp', 'expert')), may hold values from -6 to 6
- out_grad: bfloat16 [32768, 2048], P(('dp', 'expert')), may hold values from -1.5 to 1.5
- routes: int32 [32768, 2], P(('dp', 'expert')), may hold values from 0 to 15, all different within a row; in each aligned block of 128 rows (0 to 127, 128 to 255, ...) at most 32 rows name the same one
- route_probs: bfloat16 [32768, 2], P(('dp', 'expert')), may hold values from 0.049804688 to 1
- kept_count: int32 [16], P('dp'), may hold values from 512 to 2048, as said below
- gate_weight: bfloat16 [16, 2048, 768], P('expert', 'dp'), may hold values from -0.125 to 0.125
- up_weight: bfloat16 [16, 2048, 768], P('expert', 'dp'), may hold values from -0.125 to 0.125
- down_weight: bfloat16 [16, 2048, 768], P('expert', 'dp'), may hold values from -0.21875 to 0.21875
Outputs:
- token_grad: bfloat16 [32768, 2048], P(('dp', 'expert'))
- prob_grad: bfloat16 [32768, 2], P(('dp', 'expert'))
- weight_grad: bfloat16 [16, 2048, 2304], P('expert', 'dp')
The draws below stay inside these ranges and needn't reach their ends.
Inputs may be any that keep to these rules, and one draw needn't show every extreme that they name: `routes`: among the rows of one device, no expert is named more than 32 times, and a row names 2 different experts. `kept_count`: rows of a data group whose index within the group is below its count are kept; in every draw some group keeps all its rows and another keeps a quarter of them.
All inputs are finite; a program needn't handle non-finite values.
Results may differ from the reference program's by a relative error of at most 0.018.
Values may be sent and summed in bfloat16 or wider, within the bound.
No kernel may reach another device: no remote copies, remote signals or barrier semaphores. Data moves between devices by JAX's collectives and lax.ppermute only.
A program may use at most 128 MiB of HBM per device.

```python
import math
import jax
import jax.numpy as jnp
import numpy as np
from jax import lax

D = 2048
FF = 768
TOP = 2
TOK_DEV = 128
EXPERTS = 16
CAP = 32
GROUP_ROWS = 2048
TOKENS = 32768
N_DP = 16
N_EXPERT = 16


def draw_kept_count(key, part):
    counts = jax.random.randint(jax.random.fold_in(key, 11), (N_DP,), GROUP_ROWS // 4, GROUP_ROWS + 1).astype(jnp.int32)
    order = jax.random.permutation(jax.random.fold_in(key, 12), N_DP)
    counts = counts.at[order[0]].set(GROUP_ROWS)
    counts = counts.at[order[1]].set(GROUP_ROWS // 4)
    return counts.astype(jnp.int32)


def steps_of(key, dims, shards, low, top_value):
    level, own = 1.0, jax.random.fold_in(key, 6)
    for axis_at, parts in shards:
        heights = jnp.exp(jax.random.uniform(jax.random.fold_in(own, axis_at), (parts,), jnp.float32, low / len(shards), top_value / len(shards)))
        level = level * jnp.repeat(heights, dims[axis_at] // parts).reshape([-1 if axis == axis_at else 1 for axis in range(len(dims))])
    return level


def routed_block(own_key, own, number, rows, amount, top, limit, slope):
    sequence = jax.random.permutation(own_key, amount)
    crowded, common = shares(amount, rows * top, limit, slope, True), shares(amount, rows * top, limit, slope, False)
    places = jnp.arange(amount)

    def named(tallies, turn):
        used = int((tallies > 0).sum())
        fixed = max(1, used // 4)
        passed = fixed + (places - fixed + turn * (used - fixed)) % max(1, amount - fixed)
        return jnp.zeros((amount,), jnp.int32).at[sequence[jnp.where(places < fixed, places, passed)]].set(jnp.asarray(tallies, jnp.int32))

    tallies = jnp.where(number % 4 == 0, named(crowded, number // 4), named(common, number - number // 4 - 1))
    mixed = jax.random.permutation(jax.random.fold_in(own, 3), amount)
    donor, sink = mixed[0:amount // 2 * 2:2], mixed[1:amount // 2 * 2:2]
    slack = jnp.minimum(tallies[donor] - 1, limit - tallies[sink]) // 2
    slack = jnp.where((donor == sequence[0]) | (sink == sequence[0]) | (tallies[sink] == 0), 0, jnp.maximum(slack, 0))
    passed = jax.random.randint(jax.random.fold_in(own, 4), (amount // 2,), 0, 1 << 20) % (slack + 1)
    tallies = tallies.at[donor].add(-passed).at[sink].add(passed)
    members = jnp.searchsorted(jnp.cumsum(tallies), jnp.arange(rows * top), side="right").astype(jnp.int32)
    listing = members.reshape(top, rows).T
    listing = listing[jax.random.permutation(jax.random.fold_in(own, 1), rows)]
    turn = jax.random.randint(jax.random.fold_in(own, 2), (rows, 1), 0, top)
    return jnp.take_along_axis(listing, (jnp.arange(top)[None, :] + turn) % top, axis=1)


def shares(number_of, total, limit, lean, full):
    loads = [(1 << 20) // math.isqrt(grade ** lean) + 1 for grade in range(1, number_of + 1)]
    largest = limit if full else min(limit, max(-(-total // number_of), total * loads[0] // sum(loads)))
    least = 1 if total - largest >= number_of - 1 else 0
    holding, spare = [largest] + [least] * (number_of - 1), total - largest - least * (number_of - 1)
    while spare > 0:
        free = [i for i in range(1, number_of) if holding[i] < largest] or [i for i in range(1, number_of) if holding[i] < limit]
        mass, budget = sum([loads[i] for i in free]), spare
        for i in free:
            more = min(limit - holding[i], max(1, budget * loads[i] // mass), spare)
            holding[i] = holding[i] + more
            spare = spare - more
    return np.array(holding)


def bell_draw(rng, extent, deviation, reach, pieces=(), held_as=jnp.bfloat16):
    drawn = deviation * jax.random.normal(rng, extent, jnp.float32)
    if pieces:
        drawn = drawn * steps_of(rng, extent, pieces, -0.22, 0.18)
    return jnp.clip(drawn, -reach, reach).astype(held_as)


def setup_inputs(seed: int = 0) -> dict:
    arg_keys = jax.random.split(jax.random.key(seed), 9)
    tokens = bell_draw(arg_keys[0], (TOKENS, D), 1.0, 6.0, ((0, 256),))
    out_grad = bell_draw(arg_keys[1], (TOKENS, D), 0.25, 1.5, ((0, 256),))
    routes_keys = jax.random.split(jax.random.fold_in(arg_keys[2], 1), TOKENS // TOK_DEV)
    routes_turns = jax.random.permutation(jax.random.fold_in(arg_keys[2], 3), TOKENS // TOK_DEV)
    routes = jax.vmap(lambda own, number: routed_block(jax.random.fold_in(arg_keys[2], 2), own, number, TOK_DEV, EXPERTS, TOP, CAP, 2))(routes_keys, routes_turns).reshape((TOKENS, TOP))
    route_probs = jnp.clip(jnp.exp(math.log(1.0) - 2.9996462 * jax.random.uniform(arg_keys[3], (TOKENS, TOP), jnp.float32) ** steps_of(arg_keys[3], (TOKENS, TOP), ((0, 256),), -0.2, 0.2)), 0.049804688, 1.0).astype(jnp.bfloat16)
    kept_count = draw_kept_count(jax.random.fold_in(arg_keys[8], 71), 0)
    gate_weight = bell_draw(arg_keys[5], (EXPERTS, D, FF), D ** -0.5, 0.125, ((0, 16), (1, 16)))
    up_weight = bell_draw(arg_keys[6], (EXPERTS, D, FF), D ** -0.5, 0.125, ((0, 16), (1, 16)))
    down_weight = bell_draw(arg_keys[7], (EXPERTS, D, FF), FF ** -0.5, 0.21875, ((0, 16), (1, 16)))
    return {"tokens": tokens, "out_grad": out_grad, "routes": routes, "route_probs": route_probs, "kept_count": kept_count, "gate_weight": gate_weight, "up_weight": up_weight, "down_weight": down_weight}


def slot_positions(routes):
    blocks = routes.reshape(N_DP * N_EXPERT, TOK_DEV * TOP)
    onehot = (blocks[:, :, None] == jnp.arange(EXPERTS, dtype=jnp.int32)[None, None, :]).astype(jnp.int32)
    before = jnp.cumsum(onehot, axis=1) - onehot
    position = jnp.sum(before * onehot, axis=2)
    return position.reshape(TOKENS, TOP).astype(jnp.int32)


def reference(tokens, out_grad, routes, route_probs, kept_count, gate_weight, up_weight, down_weight):
    row = jnp.arange(TOKENS, dtype=jnp.int32)
    kept = (row % GROUP_ROWS) < kept_count[row // GROUP_ROWS]
    masked = jnp.where(kept[:, None], out_grad, jnp.zeros_like(out_grad))
    position = slot_positions(routes)
    block = row // TOK_DEV
    group = (block // N_EXPERT).astype(jnp.int32)
    source = (block % N_EXPERT).astype(jnp.int32)
    route_id = (row[:, None] * TOP + jnp.arange(TOP, dtype=jnp.int32)[None, :]).astype(jnp.int32)
    empty_id = TOKENS * TOP
    table = jnp.full((EXPERTS, N_DP, N_EXPERT, CAP), empty_id, jnp.int32)
    table = table.at[routes, group[:, None], source[:, None], position].set(route_id)
    flat_probs = route_probs.reshape(-1)

    def expert_step(carry, inputs):
        contrib, prob_acc = carry
        ids, w_gate, w_up, w_down = inputs
        ids = ids.reshape(-1)
        valid = ids < empty_id
        safe = jnp.where(valid, ids, 0).astype(jnp.int32)
        token_of = (safe // TOP).astype(jnp.int32)
        rows_in = jnp.where(valid[:, None], tokens[token_of], jnp.zeros((), jnp.bfloat16))
        grad_in = jnp.where(valid[:, None], masked[token_of], jnp.zeros((), jnp.bfloat16))
        prob_in = jnp.where(valid, flat_probs[safe], jnp.zeros((), jnp.bfloat16))
        pre_gate = jnp.dot(rows_in, w_gate, preferred_element_type=jnp.float32)
        pre_up = jnp.dot(rows_in, w_up, preferred_element_type=jnp.float32)
        sig = jax.nn.sigmoid(pre_gate)
        act = (pre_gate * sig * pre_up).astype(jnp.bfloat16)
        output_rows = jnp.dot(act, w_down.T, preferred_element_type=jnp.float32)
        prob_part = jnp.sum(grad_in.astype(jnp.float32) * output_rows, axis=1).astype(jnp.bfloat16)
        scaled = (prob_in.astype(jnp.float32)[:, None] * grad_in.astype(jnp.float32)).astype(jnp.bfloat16)
        back_hidden = jnp.dot(scaled, w_down, preferred_element_type=jnp.float32)
        d_gate = (back_hidden * pre_up * sig * (1.0 + pre_gate * (1.0 - sig))).astype(jnp.bfloat16)
        d_up = (back_hidden * pre_gate * sig).astype(jnp.bfloat16)
        route_back = (jnp.dot(d_gate, w_gate.T, preferred_element_type=jnp.float32)
                      + jnp.dot(d_up, w_up.T, preferred_element_type=jnp.float32)).astype(jnp.bfloat16)
        rows_g = rows_in.reshape(N_DP, N_EXPERT * CAP, D).astype(jnp.float32)
        scaled_g = scaled.reshape(N_DP, N_EXPERT * CAP, D).astype(jnp.float32)
        gate_g = d_gate.reshape(N_DP, N_EXPERT * CAP, FF).astype(jnp.float32)
        up_g = d_up.reshape(N_DP, N_EXPERT * CAP, FF).astype(jnp.float32)
        act_g = act.reshape(N_DP, N_EXPERT * CAP, FF).astype(jnp.float32)
        partial_value = jnp.concatenate((jnp.einsum('grd,grf->gdf', rows_g, gate_g),
                                   jnp.einsum('grd,grf->gdf', rows_g, up_g),
                                   jnp.einsum('grd,grf->gdf', scaled_g, act_g)), axis=2).astype(jnp.bfloat16)
        summed = jnp.sum(partial_value.astype(jnp.float32), axis=0).astype(jnp.bfloat16)
        contrib = contrib.at[ids].set(route_back, mode="drop")
        prob_acc = prob_acc.at[ids].set(prob_part, mode="drop")
        return (contrib, prob_acc), summed

    start = (jnp.zeros((TOKENS * TOP, D), jnp.bfloat16), jnp.zeros((TOKENS * TOP,), jnp.bfloat16))
    (contrib, prob_acc), weight_grad = lax.scan(expert_step, start, (table, gate_weight, up_weight, down_weight))
    token_grad = jnp.sum(contrib.reshape(TOKENS, TOP, D).astype(jnp.float32), axis=1).astype(jnp.bfloat16)
    prob_grad = prob_acc.reshape(TOKENS, TOP)
    return token_grad, prob_grad, weight_grad
```

```python
import jax
import jax.numpy as jnp
from jax import lax
from jax.sharding import PartitionSpec as P


def contract_rows(left, right):
    return lax.dot_general(
        left, right, (((0,), (0,)), ((), ())), preferred_element_type=jnp.float32
    )


def contract_last(left, right):
    return lax.dot_general(
        left, right, (((1,), (1,)), ((), ())), preferred_element_type=jnp.float32
    )


def per_device(
    tokens, out_grad, routes, route_probs, kept_count, gate_weight, up_weight, down_weight
):
    tok_rows, width = tokens.shape
    top = routes.shape[1]
    experts = lax.axis_size("expert")
    capacity = 2 * tok_rows * top // experts
    slots = experts * capacity
    weights = lax.all_gather(
        jnp.concatenate((gate_weight, up_weight, down_weight), axis=0), "dp", axis=1, tiled=True
    )
    row = lax.axis_index("expert") * tok_rows + jnp.arange(tok_rows, dtype=jnp.int32)
    kept = row < kept_count[0]
    masked = jnp.where(kept[:, None], out_grad, jnp.zeros_like(out_grad))
    flat = routes.reshape(-1)
    onehot = (flat[:, None] == jnp.arange(experts, dtype=jnp.int32)[None, :]).astype(jnp.int32)
    before = jnp.cumsum(onehot, axis=0) - onehot
    position = jnp.sum(before * onehot, axis=1)
    target = (flat * capacity + position).reshape(tok_rows, top)
    slot = jnp.arange(slots, dtype=jnp.int32)[:, None]
    probs = route_probs.astype(jnp.float32)
    match = [slot == target[None, :, k] for k in range(top)]
    placing = (match[0] | match[1]).astype(jnp.bfloat16)
    weighted = (
        jnp.where(match[0], probs[None, :, 0], 0.0) + jnp.where(match[1], probs[None, :, 1], 0.0)
    ).astype(jnp.bfloat16)
    send_rows = jnp.dot(placing, tokens, preferred_element_type=jnp.float32).astype(jnp.bfloat16)
    send_scaled = jnp.dot(weighted, masked, preferred_element_type=jnp.float32).astype(jnp.bfloat16)
    rows_in = lax.all_to_all(send_rows, "expert", split_axis=0, concat_axis=0, tiled=True)
    scaled = lax.all_to_all(send_scaled, "expert", split_axis=0, concat_axis=0, tiled=True)
    pre_gate = jnp.dot(rows_in, weights[0], preferred_element_type=jnp.float32)
    pre_up = jnp.dot(rows_in, weights[1], preferred_element_type=jnp.float32)
    sig = jax.nn.sigmoid(pre_gate)
    act = (pre_gate * sig * pre_up).astype(jnp.bfloat16)
    back_hidden = jnp.dot(scaled, weights[2], preferred_element_type=jnp.float32)
    prob_part = jnp.sum(act.astype(jnp.float32) * back_hidden, axis=1)
    d_gate = (back_hidden * pre_up * sig * (1.0 + pre_gate * (1.0 - sig))).astype(jnp.bfloat16)
    d_up = (back_hidden * pre_gate * sig).astype(jnp.bfloat16)
    weight_grad = lax.psum_scatter(
        jnp.concatenate(
            (
                contract_rows(rows_in, d_gate),
                contract_rows(rows_in, d_up),
                contract_rows(scaled, act),
            ),
            axis=1,
        ).astype(jnp.bfloat16),
        "dp",
        scatter_dimension=0,
        tiled=True,
    )[None]
    route_back = (contract_last(d_gate, weights[0]) + contract_last(d_up, weights[1])).astype(
        jnp.bfloat16
    )
    prob_all = lax.all_gather(
        prob_part.astype(jnp.bfloat16).reshape(experts, capacity), "expert", axis=0, tiled=False
    )
    rows_back = lax.all_to_all(route_back, "expert", split_axis=0, concat_axis=0, tiled=True)
    prob_back = lax.dynamic_index_in_dim(
        prob_all, lax.axis_index("expert"), axis=1, keepdims=False
    ).reshape(slots)
    token_grad = contract_rows(placing, rows_back).astype(jnp.bfloat16)
    prob_grad = jnp.stack(
        [jnp.sum(jnp.where(m, prob_back.astype(jnp.float32)[:, None], 0.0), axis=0) for m in match],
        axis=1,
    )
    prob_grad = (prob_grad / probs).astype(jnp.bfloat16)
    return (token_grad, prob_grad, weight_grad)


def solution(mesh):
    in_specs = (
        P(("dp", "expert"), None),
        P(("dp", "expert"), None),
        P(("dp", "expert"), None),
        P(("dp", "expert"), None),
        P("dp"),
        P("expert", "dp", None),
        P("expert", "dp", None),
        P("expert", "dp", None),
    )
    out_specs = (P(("dp", "expert"), None), P(("dp", "expert"), None), P("expert", "dp", None))
    return jax.shard_map(
        per_device, mesh=mesh, in_specs=in_specs, out_specs=out_specs, check_vma=False
    )
```

```python
import jax
import jax.numpy as jnp
from jax import lax
from jax.experimental import pallas as pl
from jax.experimental.pallas import tpu as pltpu
from jax.sharding import PartitionSpec as P

F32 = jnp.float32
BF16 = jnp.bfloat16
VMEM_LIMIT = 56 * 1024 * 1024
LANES = 128
BLOCK = 256


def dot(left, right):
    return jnp.dot(left, right, preferred_element_type=F32)


def dot_rows(left, right):
    return lax.dot_general(left, right, (((0,), (0,)), ((), ())), preferred_element_type=F32)


def dot_last(left, right):
    return lax.dot_general(left, right, (((1,), (1,)), ((), ())), preferred_element_type=F32)


def params():
    return pltpu.CompilerParams(
        vmem_limit_bytes=VMEM_LIMIT, dimension_semantics=("arbitrary",)
    )


def hidden(received, weights):
    experts, _, capacity, width = received.shape
    slots, ff = experts * capacity, weights.shape[2]

    def body(rows_ref, scaled_ref, w_ref, grads_ref, act_ref, prob_ref, rows_out, scaled_out):
        rows = rows_ref[...].reshape(slots, width)
        scaled = scaled_ref[...].reshape(slots, width)
        gate = dot(rows, w_ref[0])
        up = dot(rows, w_ref[1])
        back = dot(scaled, w_ref[2])
        sig = jax.nn.sigmoid(gate)
        silu = gate * sig
        act = (silu * up).astype(BF16)
        grads_ref[:, :BLOCK] = (back * up * (sig * (1.0 + gate * (1.0 - sig)))).astype(BF16)
        grads_ref[:, BLOCK:] = (back * silu).astype(BF16)
        act_ref[...] = act
        part = jnp.sum(act.astype(F32) * back, axis=1, keepdims=True)

        @pl.when(pl.program_id(0) == 0)
        def _():
            prob_ref[...] = part
            rows_out[...] = rows
            scaled_out[...] = scaled

        @pl.when(pl.program_id(0) > 0)
        def _():
            prob_ref[...] += part

    return pl.pallas_call(
        body,
        grid=(ff // BLOCK,),
        in_specs=[
            pl.BlockSpec((experts, 1, capacity, width), lambda j: (0, 0, 0, 0)),
            pl.BlockSpec((experts, 1, capacity, width), lambda j: (0, 1, 0, 0)),
            pl.BlockSpec((3, width, BLOCK), lambda j: (0, 0, j)),
        ],
        out_specs=[
            pl.BlockSpec((slots, 2 * BLOCK), lambda j: (0, j)),
            pl.BlockSpec((slots, BLOCK), lambda j: (0, j)),
            pl.BlockSpec((slots, 1), lambda j: (0, 0)),
            pl.BlockSpec((slots, width), lambda j: (0, 0)),
            pl.BlockSpec((slots, width), lambda j: (0, 0)),
        ],
        out_shape=[
            jax.ShapeDtypeStruct((slots, 2 * ff), BF16),
            jax.ShapeDtypeStruct((slots, ff), BF16),
            jax.ShapeDtypeStruct((slots, 1), F32),
            jax.ShapeDtypeStruct((slots, width), BF16),
            jax.ShapeDtypeStruct((slots, width), BF16),
        ],
        compiler_params=params(),
        name="hidden",
    )(received, received, weights)


def route_back(grads, weights, prob):
    slots, width, ff = grads.shape[0], *weights.shape[1:]
    steps = width // BLOCK

    def body(grads_ref, w_ref, prob_ref, out_ref):
        @pl.when(pl.program_id(0) < steps)
        def _():
            value = jnp.zeros((slots, BLOCK), F32)
            for j in range(ff // BLOCK):
                for n in range(2):
                    at = (2 * j + n) * BLOCK
                    value += dot_last(
                        grads_ref[:, at : at + BLOCK], w_ref[n, :, j * BLOCK : (j + 1) * BLOCK]
                    )
            out_ref[...] = value.astype(BF16)

        @pl.when(pl.program_id(0) == steps)
        def _():
            out_ref[...] = jnp.broadcast_to(prob_ref[...], (slots, BLOCK)).astype(BF16)

    return pl.pallas_call(
        body,
        grid=(steps + 1,),
        in_specs=[
            pl.BlockSpec((slots, 2 * ff), lambda i: (0, 0)),
            pl.BlockSpec((2, BLOCK, ff), lambda i: (0, jnp.minimum(i, steps - 1), 0)),
            pl.BlockSpec((slots, 1), lambda i: (0, 0)),
        ],
        out_specs=pl.BlockSpec((slots, BLOCK), lambda i: (0, i)),
        out_shape=jax.ShapeDtypeStruct((slots, width + BLOCK), BF16),
        compiler_params=params(),
        name="route_back",
    )(grads, weights, prob)


def per_device(
    tokens, out_grad, routes, route_probs, kept_count, gate_weight, up_weight, down_weight
):
    tok_rows, width = tokens.shape
    top = routes.shape[1]
    experts = lax.axis_size("expert")
    chips = lax.axis_size("dp") // 2
    capacity = 2 * tok_rows * top // experts
    slots = experts * capacity
    ff = gate_weight.shape[2]
    dp = lax.axis_index("dp")
    chip, core = dp // 2, dp % 2
    swap = [(2 * z + c, 2 * z + 1 - c) for z in range(chips) for c in range(2)]
    up_ring = [(2 * z + c, 2 * ((z + 1) % chips) + c) for z in range(chips) for c in range(2)]
    down_ring = [(2 * z + c, 2 * ((z - 1) % chips) + c) for z in range(chips) for c in range(2)]

    weights = lax.all_gather(
        jnp.concatenate((gate_weight, up_weight, down_weight), axis=0), "dp", axis=1, tiled=True
    )

    row = lax.axis_index("expert") * tok_rows + jnp.arange(tok_rows, dtype=jnp.int32)
    kept = row < kept_count[0]
    flat = routes.reshape(-1)
    onehot = (flat[:, None] == jnp.arange(experts, dtype=jnp.int32)[None, :]).astype(jnp.int32)
    before = jnp.cumsum(onehot, axis=0) - onehot
    position = jnp.sum(before * onehot, axis=1)
    target = (flat * capacity + position).reshape(tok_rows, top)
    probs = route_probs.astype(F32)
    factor = jnp.where(kept[:, None], probs, 0.0)
    line = jnp.arange(2 * slots, dtype=jnp.int32)[:, None]
    line_slot = line // (2 * capacity) * capacity + line % capacity
    line_half = line // capacity % 2
    twice = jnp.concatenate((target, target), axis=0)
    factor = jnp.concatenate((jnp.ones_like(probs), factor), axis=0)
    side = (jnp.arange(2 * tok_rows, dtype=jnp.int32) // tok_rows)[None, :]
    spread = sum(
        jnp.where((line_slot == twice[None, :, k]) & (line_half == side), factor[None, :, k], 0.0)
        for k in range(top)
    ).astype(BF16)
    send = dot(spread, jnp.concatenate((tokens, out_grad), axis=0)).astype(BF16)

    def exchange(value, lines):
        return lax.all_to_all(
            value.reshape(experts, lines, -1), "expert", split_axis=0, concat_axis=0, tiled=True
        )

    far = chips // 2
    at = [(chip + n) % chips for n in range(chips)]
    send, at, core, target = lax.optimization_barrier((send, at, core, target))
    received, at, core, target = lax.optimization_barrier(
        (exchange(send, 2 * capacity), at, core, target)
    )
    grads, act, prob_part, rows_in, scaled = hidden(
        received.reshape(experts, 2, capacity, width), weights
    )

    def add(*values):
        return sum(value.astype(F32) for value in values).astype(BF16)

    def block(part, n, side):
        return lax.dynamic_slice(part, (at[n], side, 0, 0), (1, 1, *part.shape[2:]))[0, 0]

    def half(part, side):
        return lax.dynamic_slice(part, (0, side, 0, 0), (chips, 1, *part.shape[2:]))[:, 0]

    down_part = dot_rows(scaled, act).astype(BF16).reshape(chips, 2, LANES, ff)
    down_other = lax.ppermute(half(down_part, 1 - core), "dp", swap)
    rows_in, down_part = lax.optimization_barrier((rows_in, down_part))
    gate_up = dot_rows(rows_in, grads).astype(BF16).reshape(chips, 2, LANES, 2 * ff)
    far_other = lax.ppermute(block(gate_up, far, 1 - core), "dp", swap)
    down_pair = add(half(down_part, core), down_other).reshape(chips * LANES, ff)
    gate_up, down_pair, far_other = lax.optimization_barrier((gate_up, down_pair, far_other))
    down_sum = lax.psum_scatter(
        down_pair,
        "dp",
        scatter_dimension=0,
        axis_index_groups=[[2 * z + c for z in range(chips)] for c in range(2)],
        tiled=True,
    )
    far_sum = add(block(gate_up, far, core), far_other)

    def both_ways(right, left):
        right, left = lax.optimization_barrier((right, left))
        right, left = lax.ppermute(right, "dp", up_ring), lax.ppermute(left, "dp", down_ring)
        return lax.optimization_barrier((right, left))

    def pair(n):
        return add(
            block(gate_up, n, core), lax.dynamic_slice(other, (at[n], 0, 0), (1, LANES, 2 * ff))[0]
        )

    grads, gate_up, far_sum = lax.optimization_barrier((grads, gate_up, far_sum))
    other = lax.ppermute(half(gate_up, 1 - core), "dp", swap)
    right, left = both_ways(far_sum[:, :ff], far_sum[:, ff:])
    back = route_back(grads, weights, prob_part)
    right, left, back = lax.optimization_barrier((right, left, back))
    zeros = jnp.zeros((LANES, ff), BF16)
    right = jnp.concatenate((right, zeros), axis=1)
    left = jnp.concatenate((zeros, left), axis=1)
    for n in range(far - 1, 0, -1):
        if n == 1:
            right, left, down_sum = lax.optimization_barrier((right, left, down_sum))
        right, left = both_ways(add(pair(n), right), add(pair(chips - n), left))
    back, right, left = lax.optimization_barrier((exchange(back, capacity), right, left))
    total = add(pair(0), right, left)
    columns = [
        total[:, (2 * j + n) * BLOCK : (2 * j + n + 1) * BLOCK]
        for n in range(2)
        for j in range(ff // BLOCK)
    ]
    weight_grad = jnp.concatenate((*columns, down_sum), axis=1)[None]

    back = back.reshape(slots, width + BLOCK)
    slot = jnp.arange(slots, dtype=jnp.int32)[:, None]
    match = [slot == target[None, :, k] for k in range(top)]
    placing = (match[0] | match[1]).astype(BF16)
    token_grad = dot_rows(placing, back[:, :width]).astype(BF16)
    prob_back = back[:, width].astype(F32)
    prob_grad = jnp.stack(
        [jnp.sum(jnp.where(m, prob_back[:, None], 0.0), axis=0) for m in match], axis=1
    )
    prob_grad = (prob_grad / probs).astype(BF16)
    return (token_grad, prob_grad, weight_grad)


def solution(mesh):
    in_specs = (
        P(("dp", "expert"), None),
        P(("dp", "expert"), None),
        P(("dp", "expert"), None),
        P(("dp", "expert"), None),
        P("dp"),
        P("expert", "dp", None),
        P("expert", "dp", None),
        P("expert", "dp", None),
    )
    out_specs = (P(("dp", "expert"), None), P(("dp", "expert"), None), P("expert", "dp", None))
    return jax.shard_map(
        per_device, mesh=mesh, in_specs=in_specs, out_specs=out_specs, check_vma=False
    )
```

```python
import jax
import jax.numpy as jnp
from jax import lax
from jax.experimental import pallas as pl
from jax.experimental.pallas import tpu as pltpu
from jax.sharding import PartitionSpec as P

F32 = jnp.float32
BF16 = jnp.bfloat16
VMEM_LIMIT = 56 * 1024 * 1024
LANES = 128
BLOCK = 256


def dot(left, right):
    return jnp.dot(left, right, preferred_element_type=F32)


def dot_rows(left, right):
    return lax.dot_general(left, right, (((0,), (0,)), ((), ())), preferred_element_type=F32)


def dot_last(left, right):
    return lax.dot_general(left, right, (((1,), (1,)), ((), ())), preferred_element_type=F32)


def params():
    return pltpu.CompilerParams(
        vmem_limit_bytes=VMEM_LIMIT, dimension_semantics=("arbitrary",)
    )


def hidden(received, weights, core):
    experts, _, capacity, width = received.shape
    slots, ff = experts * capacity, weights.shape[2]

    def body(s_ref, rows_ref, scaled_ref, w_ref, grads_ref, act_ref, prob_ref, *apart):
        rows = rows_ref[...].reshape(slots, width)
        scaled = scaled_ref[...].reshape(slots, width)
        gate = dot(rows, w_ref[0])
        up = dot(rows, w_ref[1])
        back = dot(scaled, w_ref[2])
        sig = jax.nn.sigmoid(gate)
        silu = gate * sig
        act = (silu * up).astype(BF16)
        d_gate = (back * up * (sig * (1.0 + gate * (1.0 - sig)))).astype(BF16)
        d_up = (back * silu).astype(BF16)
        for j in range(ff // BLOCK):

            @pl.when(pl.program_id(0) == j)
            def _():
                grads_ref[:, j * BLOCK : (j + 1) * BLOCK] = d_gate
                grads_ref[:, ff + j * BLOCK : ff + (j + 1) * BLOCK] = d_up

        act_ref[...] = act
        part = jnp.sum(act.astype(F32) * back, axis=1, keepdims=True)

        @pl.when(pl.program_id(0) == 0)
        def _():
            prob_ref[...] = part
            first = s_ref[0] == 0
            for value, own_ref, other_ref in ((rows, *apart[:2]), (scaled, *apart[2:])):
                for n in range(width // (2 * LANES)):
                    at = slice(n * LANES, (n + 1) * LANES)
                    low = value[:, 2 * n * LANES : (2 * n + 1) * LANES]
                    high = value[:, (2 * n + 1) * LANES : (2 * n + 2) * LANES]
                    own_ref[:, at] = jnp.where(first, low, high)
                    other_ref[:, at] = jnp.where(first, high, low)

        @pl.when(pl.program_id(0) > 0)
        def _():
            prob_ref[...] += part

    return pl.pallas_call(
        body,
        grid_spec=pltpu.PrefetchScalarGridSpec(
            num_scalar_prefetch=1,
            grid=(ff // BLOCK,),
            in_specs=[
                pl.BlockSpec((experts, 1, capacity, width), lambda j, s: (0, 0, 0, 0)),
                pl.BlockSpec((experts, 1, capacity, width), lambda j, s: (0, 1, 0, 0)),
                pl.BlockSpec((3, width, BLOCK), lambda j, s: (0, 0, j)),
            ],
            out_specs=[
                pl.BlockSpec((slots, 2 * ff), lambda j, s: (0, 0)),
                pl.BlockSpec((slots, BLOCK), lambda j, s: (0, j)),
                pl.BlockSpec((slots, 1), lambda j, s: (0, 0)),
            ]
            + [pl.BlockSpec((slots, width // 2), lambda j, s: (0, 0))] * 4,
        ),
        out_shape=[
            jax.ShapeDtypeStruct((slots, 2 * ff), BF16),
            jax.ShapeDtypeStruct((slots, ff), BF16),
            jax.ShapeDtypeStruct((slots, 1), F32),
        ]
        + [jax.ShapeDtypeStruct((slots, width // 2), BF16)] * 4,
        compiler_params=params(),
        name="hidden",
    )(core[None].astype(jnp.int32), received, received, weights)


def route_back(grads, weights, prob):
    slots, width, ff = grads.shape[0], *weights.shape[1:]
    steps = width // BLOCK

    def body(grads_ref, w_ref, prob_ref, out_ref):
        @pl.when(pl.program_id(0) < steps)
        def _():
            value = dot_last(grads_ref[:, :ff], w_ref[0]) + dot_last(grads_ref[:, ff:], w_ref[1])
            out_ref[...] = value.astype(BF16)

        @pl.when(pl.program_id(0) == steps)
        def _():
            out_ref[...] = jnp.broadcast_to(prob_ref[...], (slots, BLOCK)).astype(BF16)

    return pl.pallas_call(
        body,
        grid=(steps + 1,),
        in_specs=[
            pl.BlockSpec((slots, 2 * ff), lambda i: (0, 0)),
            pl.BlockSpec((2, BLOCK, ff), lambda i: (0, jnp.minimum(i, steps - 1), 0)),
            pl.BlockSpec((slots, 1), lambda i: (0, 0)),
        ],
        out_specs=pl.BlockSpec((slots, BLOCK), lambda i: (0, i)),
        out_shape=jax.ShapeDtypeStruct((slots, width + BLOCK), BF16),
        compiler_params=params(),
        name="route_back",
    )(grads, weights, prob)


def per_device(
    tokens, out_grad, routes, route_probs, kept_count, gate_weight, up_weight, down_weight
):
    tok_rows, width = tokens.shape
    top = routes.shape[1]
    experts = lax.axis_size("expert")
    chips = lax.axis_size("dp") // 2
    capacity = 2 * tok_rows * top // experts
    slots = experts * capacity
    ff = gate_weight.shape[2]
    dp = lax.axis_index("dp")
    chip, core = dp // 2, dp % 2
    swap = [(2 * z + c, 2 * z + 1 - c) for z in range(chips) for c in range(2)]
    up_ring = [(2 * z + c, 2 * ((z + 1) % chips) + c) for z in range(chips) for c in range(2)]
    down_ring = [(2 * z + c, 2 * ((z - 1) % chips) + c) for z in range(chips) for c in range(2)]

    weights = lax.all_gather(
        jnp.concatenate((gate_weight, up_weight, down_weight), axis=0), "dp", axis=1, tiled=True
    )

    row = lax.axis_index("expert") * tok_rows + jnp.arange(tok_rows, dtype=jnp.int32)
    kept = row < kept_count[0]
    flat = routes.reshape(-1)
    onehot = (flat[:, None] == jnp.arange(experts, dtype=jnp.int32)[None, :]).astype(jnp.int32)
    before = jnp.cumsum(onehot, axis=0) - onehot
    position = jnp.sum(before * onehot, axis=1)
    target = (flat * capacity + position).reshape(tok_rows, top)
    probs = route_probs.astype(F32)
    factor = jnp.where(kept[:, None], probs, 0.0)
    line = jnp.arange(2 * slots, dtype=jnp.int32)[:, None]
    line_slot = line // (2 * capacity) * capacity + line % capacity
    line_half = line // capacity % 2
    twice = jnp.concatenate((target, target), axis=0)
    factor = jnp.concatenate((jnp.ones_like(probs), factor), axis=0)
    side = (jnp.arange(2 * tok_rows, dtype=jnp.int32) // tok_rows)[None, :]
    spread = sum(
        jnp.where((line_slot == twice[None, :, k]) & (line_half == side), factor[None, :, k], 0.0)
        for k in range(top)
    ).astype(BF16)
    send = dot(spread, jnp.concatenate((tokens, out_grad), axis=0)).astype(BF16)

    def exchange(value, lines):
        return lax.all_to_all(
            value.reshape(experts, lines, -1), "expert", split_axis=0, concat_axis=0, tiled=True
        )

    far = chips // 2
    at = [(chip + n) % chips for n in range(chips)]
    send, at, core, target = lax.optimization_barrier((send, at, core, target))
    received, at, core, target = lax.optimization_barrier(
        (exchange(send, 2 * capacity), at, core, target)
    )
    grads, act, prob_part, rows_own, rows_other, scaled_own, scaled_other = hidden(
        received.reshape(experts, 2, capacity, width), weights, core
    )

    def add(*values):
        return sum(value.astype(F32) for value in values).astype(BF16)

    def swapped(value):
        return lax.ppermute(value, "dp", swap)

    def grad_of(left, right):
        return dot_rows(left, right).astype(BF16)

    def both_ways(right, left):
        right, left = lax.optimization_barrier((right, left))
        right, left = lax.ppermute(right, "dp", up_ring), lax.ppermute(left, "dp", down_ring)
        return lax.optimization_barrier((right, left))

    gate_up_other = swapped(grad_of(rows_other, grads))
    far_own, far_other = (
        grad_of(lax.dynamic_slice(lines, (0, at[far] * LANES), (slots, LANES)), act)
        for lines in (scaled_own, scaled_other)
    )
    far_other = swapped(far_other)
    other = swapped(grad_of(scaled_other, act))
    gate_up_own = grad_of(rows_own, grads)
    gate_up_own, gate_up_other, far_own, far_other, other = lax.optimization_barrier(
        (gate_up_own, gate_up_other, far_own, far_other, other)
    )
    gate_up_pair = add(gate_up_own, gate_up_other)
    far_sum = add(far_own, far_other)
    gate_up_pair, far_sum, scaled_own, grads = lax.optimization_barrier(
        (gate_up_pair, far_sum, scaled_own, grads)
    )
    gate_up_sum = lax.psum_scatter(
        gate_up_pair,
        "dp",
        scatter_dimension=0,
        axis_index_groups=[[2 * z + c for z in range(chips)] for c in range(2)],
        tiled=True,
    )
    right, left = both_ways(far_sum[: LANES // 2], far_sum[LANES // 2 :])
    own = grad_of(scaled_own, act)
    back = route_back(grads, weights, prob_part)
    right, left, back = lax.optimization_barrier((right, left, back))

    def pair(n):
        where, size = (at[n] * LANES, 0), (LANES, ff)
        return add(lax.dynamic_slice(own, where, size), lax.dynamic_slice(other, where, size))

    zeros = jnp.zeros((LANES // 2, ff), BF16)
    right = jnp.concatenate((right, zeros), axis=0)
    left = jnp.concatenate((zeros, left), axis=0)
    for n in range(far - 1, 0, -1):
        right, left = add(pair(n), right), add(pair(chips - n), left)
        if n == far - 1:
            right, left, back = lax.optimization_barrier((right, left, back))
            back = exchange(back, capacity)
        right, left = both_ways(right, left)
    down_sum = add(pair(0), right, left)
    down_sum, gate_up_sum = lax.optimization_barrier((down_sum, gate_up_sum))
    weight_grad = jnp.concatenate((gate_up_sum, down_sum), axis=1)[None]

    back = back.reshape(slots, width + BLOCK)
    slot = jnp.arange(slots, dtype=jnp.int32)[:, None]
    match = [slot == target[None, :, k] for k in range(top)]
    placing = (match[0] | match[1]).astype(BF16)
    token_grad = dot_rows(placing, back[:, :width]).astype(BF16)
    prob_back = back[:, width].astype(F32)
    prob_grad = jnp.stack(
        [jnp.sum(jnp.where(m, prob_back[:, None], 0.0), axis=0) for m in match], axis=1
    )
    prob_grad = (prob_grad / probs).astype(BF16)
    return (token_grad, prob_grad, weight_grad)


def solution(mesh):
    in_specs = (
        P(("dp", "expert"), None),
        P(("dp", "expert"), None),
        P(("dp", "expert"), None),
        P(("dp", "expert"), None),
        P("dp"),
        P("expert", "dp", None),
        P("expert", "dp", None),
        P("expert", "dp", None),
    )
    out_specs = (P(("dp", "expert"), None), P(("dp", "expert"), None), P("expert", "dp", None))
    return jax.shard_map(
        per_device, mesh=mesh, in_specs=in_specs, out_specs=out_specs, check_vma=False
    )
```

```python
import jax
import jax.numpy as jnp
from jax import lax
from jax.experimental import pallas as pl
from jax.experimental.pallas import tpu as pltpu
from jax.sharding import PartitionSpec as P

F32 = jnp.float32
BF16 = jnp.bfloat16
VMEM_LIMIT = 56 * 1024 * 1024
LANES = 128
BLOCK = 256


def dot(left, right):
    return jnp.dot(left, right, preferred_element_type=F32)


def dot_rows(left, right):
    return lax.dot_general(left, right, (((0,), (0,)), ((), ())), preferred_element_type=F32)


def dot_last(left, right):
    return lax.dot_general(left, right, (((1,), (1,)), ((), ())), preferred_element_type=F32)


def params():
    return pltpu.CompilerParams(
        vmem_limit_bytes=VMEM_LIMIT, dimension_semantics=("arbitrary",)
    )


def hidden(received, weights, core):
    experts, _, capacity, width = received.shape
    slots, ff = experts * capacity, weights.shape[2]

    def body(s_ref, rows_ref, scaled_ref, w_ref, gate_ref, up_ref, act_ref, prob_ref, *apart):
        rows = rows_ref[...].reshape(slots, width)
        scaled = scaled_ref[...].reshape(slots, width)
        gate = dot(rows, w_ref[0])
        up = dot(rows, w_ref[1])
        back = dot(scaled, w_ref[2])
        sig = jax.nn.sigmoid(gate)
        silu = gate * sig
        act = (silu * up).astype(BF16)
        gate_ref[...] = (back * up * (sig * (1.0 + gate * (1.0 - sig)))).astype(BF16)
        up_ref[...] = (back * silu).astype(BF16)
        act_ref[...] = act
        part = jnp.sum(act.astype(F32) * back, axis=1, keepdims=True)

        @pl.when(pl.program_id(0) == 0)
        def _():
            prob_ref[...] = part
            first = s_ref[0] == 0
            for value, own_ref, other_ref in ((rows, *apart[:2]), (scaled, *apart[2:])):
                for n in range(width // (2 * LANES)):
                    at = slice(n * LANES, (n + 1) * LANES)
                    low = value[:, 2 * n * LANES : (2 * n + 1) * LANES]
                    high = value[:, (2 * n + 1) * LANES : (2 * n + 2) * LANES]
                    own_ref[:, at] = jnp.where(first, low, high)
                    other_ref[:, at] = jnp.where(first, high, low)

        @pl.when(pl.program_id(0) > 0)
        def _():
            prob_ref[...] += part

    return pl.pallas_call(
        body,
        grid_spec=pltpu.PrefetchScalarGridSpec(
            num_scalar_prefetch=1,
            grid=(ff // BLOCK,),
            in_specs=[
                pl.BlockSpec((experts, 1, capacity, width), lambda j, s: (0, 0, 0, 0)),
                pl.BlockSpec((experts, 1, capacity, width), lambda j, s: (0, 1, 0, 0)),
                pl.BlockSpec((3, width, BLOCK), lambda j, s: (0, 0, j)),
            ],
            out_specs=[
                pl.BlockSpec((slots, BLOCK), lambda j, s: (0, j)),
                pl.BlockSpec((slots, BLOCK), lambda j, s: (0, j)),
                pl.BlockSpec((slots, BLOCK), lambda j, s: (0, j)),
                pl.BlockSpec((slots, 1), lambda j, s: (0, 0)),
            ]
            + [pl.BlockSpec((slots, width // 2), lambda j, s: (0, 0))] * 4,
        ),
        out_shape=[
            jax.ShapeDtypeStruct((slots, ff), BF16),
            jax.ShapeDtypeStruct((slots, ff), BF16),
            jax.ShapeDtypeStruct((slots, ff), BF16),
            jax.ShapeDtypeStruct((slots, 1), F32),
        ]
        + [jax.ShapeDtypeStruct((slots, width // 2), BF16)] * 4,
        compiler_params=params(),
        name="hidden",
    )(core[None].astype(jnp.int32), received, received, weights)


def route_back(d_gate, d_up, weights, prob):
    slots, width, ff = d_gate.shape[0], *weights.shape[1:]
    steps = width // BLOCK

    def body(gate_ref, up_ref, w_ref, prob_ref, out_ref):
        @pl.when(pl.program_id(0) < steps)
        def _():
            value = dot_last(gate_ref[...], w_ref[0]) + dot_last(up_ref[...], w_ref[1])
            out_ref[...] = value.astype(BF16)

        @pl.when(pl.program_id(0) == steps)
        def _():
            out_ref[...] = jnp.broadcast_to(prob_ref[...], (slots, BLOCK)).astype(BF16)

    return pl.pallas_call(
        body,
        grid=(steps + 1,),
        in_specs=[
            pl.BlockSpec((slots, ff), lambda i: (0, 0)),
            pl.BlockSpec((slots, ff), lambda i: (0, 0)),
            pl.BlockSpec((2, BLOCK, ff), lambda i: (0, jnp.minimum(i, steps - 1), 0)),
            pl.BlockSpec((slots, 1), lambda i: (0, 0)),
        ],
        out_specs=pl.BlockSpec((slots, BLOCK), lambda i: (0, i)),
        out_shape=jax.ShapeDtypeStruct((slots, width + BLOCK), BF16),
        compiler_params=params(),
        name="route_back",
    )(d_gate, d_up, weights, prob)


def per_device(
    tokens, out_grad, routes, route_probs, kept_count, gate_weight, up_weight, down_weight
):
    tok_rows, width = tokens.shape
    top = routes.shape[1]
    experts = lax.axis_size("expert")
    chips = lax.axis_size("dp") // 2
    capacity = 2 * tok_rows * top // experts
    slots = experts * capacity
    ff = gate_weight.shape[2]
    dp = lax.axis_index("dp")
    core = dp % 2
    swap = [(2 * z + c, 2 * z + 1 - c) for z in range(chips) for c in range(2)]

    weights = lax.all_gather(
        jnp.concatenate((gate_weight, up_weight, down_weight), axis=0), "dp", axis=1, tiled=True
    )

    row = lax.axis_index("expert") * tok_rows + jnp.arange(tok_rows, dtype=jnp.int32)
    kept = row < kept_count[0]
    flat = routes.reshape(-1)
    onehot = (flat[:, None] == jnp.arange(experts, dtype=jnp.int32)[None, :]).astype(jnp.int32)
    before = jnp.cumsum(onehot, axis=0) - onehot
    position = jnp.sum(before * onehot, axis=1)
    target = (flat * capacity + position).reshape(tok_rows, top)
    probs = route_probs.astype(F32)
    factor = jnp.where(kept[:, None], probs, 0.0)
    line = jnp.arange(2 * slots, dtype=jnp.int32)[:, None]
    line_slot = line // (2 * capacity) * capacity + line % capacity
    line_half = line // capacity % 2
    twice = jnp.concatenate((target, target), axis=0)
    factor = jnp.concatenate((jnp.ones_like(probs), factor), axis=0)
    side = (jnp.arange(2 * tok_rows, dtype=jnp.int32) // tok_rows)[None, :]
    spread = sum(
        jnp.where((line_slot == twice[None, :, k]) & (line_half == side), factor[None, :, k], 0.0)
        for k in range(top)
    ).astype(BF16)
    send = dot(spread, jnp.concatenate((tokens, out_grad), axis=0)).astype(BF16)

    def exchange(value, lines):
        return lax.all_to_all(
            value.reshape(experts, lines, -1), "expert", split_axis=0, concat_axis=0, tiled=True
        )

    send, core, target = lax.optimization_barrier((send, core, target))
    received, core, target = lax.optimization_barrier(
        (exchange(send, 2 * capacity), core, target)
    )
    d_gate, d_up, act, prob_part, rows_own, rows_other, scaled_own, scaled_other = hidden(
        received.reshape(experts, 2, capacity, width), weights, core
    )

    def add(*values):
        return sum(value.astype(F32) for value in values).astype(BF16)

    def swapped(value):
        return lax.ppermute(value, "dp", swap)

    def grad_of(left, right):
        return dot_rows(left, right).astype(BF16)

    other = []
    for lines, grad in ((scaled_other, act), (rows_other, d_gate), (rows_other, d_up)):
        if other:
            lines, grad, other[-1] = lax.optimization_barrier((lines, grad, other[-1]))
        other.append(grad_of(lines, grad))
    other = [swapped(part) for part in other]
    own_other = other
    own = [
        grad_of(lines, grad) for lines, grad in ((scaled_own, act), (rows_own, d_gate), (rows_own, d_up))
    ]
    pairs = jnp.zeros((chips * LANES, 3 * ff), BF16)
    for n, mine, theirs in zip((2, 0, 1), own, own_other, strict=True):
        pairs = lax.dynamic_update_slice(pairs, add(mine, theirs), (0, n * ff))
    weight_grad = lax.psum_scatter(
        pairs,
        "dp",
        scatter_dimension=0,
        axis_index_groups=[[2 * z + c for z in range(chips)] for c in range(2)],
        tiled=True,
    )[None]
    back = exchange(route_back(d_gate, d_up, weights, prob_part), capacity)

    back = back.reshape(slots, width + BLOCK)
    slot = jnp.arange(slots, dtype=jnp.int32)[:, None]
    match = [slot == target[None, :, k] for k in range(top)]
    placing = (match[0] | match[1]).astype(BF16)
    token_grad = dot_rows(placing, back[:, :width]).astype(BF16)
    prob_back = back[:, width].astype(F32)
    prob_grad = jnp.stack(
        [jnp.sum(jnp.where(m, prob_back[:, None], 0.0), axis=0) for m in match], axis=1
    )
    prob_grad = (prob_grad / probs).astype(BF16)
    return (token_grad, prob_grad, weight_grad)


def solution(mesh):
    in_specs = (
        P(("dp", "expert"), None),
        P(("dp", "expert"), None),
        P(("dp", "expert"), None),
        P(("dp", "expert"), None),
        P("dp"),
        P("expert", "dp", None),
        P("expert", "dp", None),
        P("expert", "dp", None),
    )
    out_specs = (P(("dp", "expert"), None), P(("dp", "expert"), None), P("expert", "dp", None))
    return jax.shard_map(
        per_device, mesh=mesh, in_specs=in_specs, out_specs=out_specs, check_vma=False
    )
```

```python
import jax
import jax.numpy as jnp
from jax import lax
from jax.experimental import pallas as pl
from jax.experimental.pallas import tpu as pltpu
from jax.sharding import PartitionSpec as P

F32 = jnp.float32
BF16 = jnp.bfloat16
VMEM_LIMIT = 56 * 1024 * 1024
LANES = 128
BLOCK = 256


def dot(left, right):
    return jnp.dot(left, right, preferred_element_type=F32)


def dot_rows(left, right):
    return lax.dot_general(left, right, (((0,), (0,)), ((), ())), preferred_element_type=F32)


def dot_last(left, right):
    return lax.dot_general(left, right, (((1,), (1,)), ((), ())), preferred_element_type=F32)


def params():
    return pltpu.CompilerParams(
        vmem_limit_bytes=VMEM_LIMIT, dimension_semantics=("arbitrary",)
    )


def hidden(received, weights, core):
    experts, _, capacity, width = received.shape
    slots, ff = experts * capacity, weights.shape[2]

    def body(s_ref, rows_ref, scaled_ref, w_ref, gate_ref, up_ref, act_ref, prob_ref, *apart):
        rows = rows_ref[...].reshape(slots, width)
        scaled = scaled_ref[...].reshape(slots, width)
        gate = dot(rows, w_ref[0])
        up = dot(rows, w_ref[1])
        back = dot(scaled, w_ref[2])
        sig = jax.nn.sigmoid(gate)
        silu = gate * sig
        act = (silu * up).astype(BF16)
        d_gate = (back * up * (sig * (1.0 + gate * (1.0 - sig)))).astype(BF16)
        d_up = (back * silu).astype(BF16)
        for j in range(ff // BLOCK):

            @pl.when(pl.program_id(0) == j)
            def _():
                at = slice(j * BLOCK, (j + 1) * BLOCK)
                gate_ref[:, at] = d_gate
                up_ref[:, at] = d_up
                act_ref[:, at] = act

        part = jnp.sum(act.astype(F32) * back, axis=1, keepdims=True)

        @pl.when(pl.program_id(0) == 0)
        def _():
            prob_ref[...] = part
            first = s_ref[0] == 0
            for value, own_ref, other_ref in ((rows, *apart[:2]), (scaled, *apart[2:])):
                for n in range(width // (2 * LANES)):
                    at = slice(n * LANES, (n + 1) * LANES)
                    low = value[:, 2 * n * LANES : (2 * n + 1) * LANES]
                    high = value[:, (2 * n + 1) * LANES : (2 * n + 2) * LANES]
                    own_ref[:, at] = jnp.where(first, low, high)
                    other_ref[:, at] = jnp.where(first, high, low)

        @pl.when(pl.program_id(0) > 0)
        def _():
            prob_ref[...] += part

    return pl.pallas_call(
        body,
        grid_spec=pltpu.PrefetchScalarGridSpec(
            num_scalar_prefetch=1,
            grid=(ff // BLOCK,),
            in_specs=[
                pl.BlockSpec((experts, 1, capacity, width), lambda j, s: (0, 0, 0, 0)),
                pl.BlockSpec((experts, 1, capacity, width), lambda j, s: (0, 1, 0, 0)),
                pl.BlockSpec((3, width, BLOCK), lambda j, s: (0, 0, j)),
            ],
            out_specs=[pl.BlockSpec(memory_space=pltpu.VMEM)] * 3
            + [pl.BlockSpec((slots, 1), lambda j, s: (0, 0))]
            + [pl.BlockSpec(memory_space=pltpu.VMEM)] * 4,
        ),
        out_shape=[pltpu.VMEM((slots, ff), BF16)] * 3
        + [jax.ShapeDtypeStruct((slots, 1), F32)]
        + [pltpu.VMEM((slots, width // 2), BF16)] * 4,
        compiler_params=params(),
        name="hidden",
    )(core[None].astype(jnp.int32), received, received, weights)


def route_back(d_gate, d_up, weights, prob):
    slots, width, ff = d_gate.shape[0], *weights.shape[1:]
    steps = width // BLOCK

    def body(gate_ref, up_ref, w_ref, prob_ref, out_ref):
        @pl.when(pl.program_id(0) < steps)
        def _():
            value = dot_last(gate_ref[...], w_ref[0]) + dot_last(up_ref[...], w_ref[1])
            out_ref[...] = value.astype(BF16)

        @pl.when(pl.program_id(0) == steps)
        def _():
            out_ref[...] = jnp.broadcast_to(prob_ref[...], (slots, BLOCK)).astype(BF16)

    return pl.pallas_call(
        body,
        grid=(steps + 1,),
        in_specs=[
            pl.BlockSpec((slots, ff), lambda i: (0, 0)),
            pl.BlockSpec((slots, ff), lambda i: (0, 0)),
            pl.BlockSpec((2, BLOCK, ff), lambda i: (0, jnp.minimum(i, steps - 1), 0)),
            pl.BlockSpec((slots, 1), lambda i: (0, 0)),
        ],
        out_specs=pl.BlockSpec((slots, BLOCK), lambda i: (0, i)),
        out_shape=jax.ShapeDtypeStruct((slots, width + BLOCK), BF16),
        compiler_params=params(),
        name="route_back",
    )(d_gate, d_up, weights, prob)


def per_device(
    tokens, out_grad, routes, route_probs, kept_count, gate_weight, up_weight, down_weight
):
    tok_rows, width = tokens.shape
    top = routes.shape[1]
    experts = lax.axis_size("expert")
    chips = lax.axis_size("dp") // 2
    capacity = 2 * tok_rows * top // experts
    slots = experts * capacity
    ff = gate_weight.shape[2]
    dp = lax.axis_index("dp")
    core = dp % 2
    swap = [(2 * z + c, 2 * z + 1 - c) for z in range(chips) for c in range(2)]

    weights = lax.all_gather(
        jnp.concatenate((gate_weight, up_weight, down_weight), axis=0), "dp", axis=1, tiled=True
    )

    row = lax.axis_index("expert") * tok_rows + jnp.arange(tok_rows, dtype=jnp.int32)
    kept = row < kept_count[0]
    flat = routes.reshape(-1)
    onehot = (flat[:, None] == jnp.arange(experts, dtype=jnp.int32)[None, :]).astype(jnp.int32)
    before = jnp.cumsum(onehot, axis=0) - onehot
    position = jnp.sum(before * onehot, axis=1)
    target = (flat * capacity + position).reshape(tok_rows, top)
    probs = route_probs.astype(F32)
    factor = jnp.where(kept[:, None], probs, 0.0)
    line = jnp.arange(2 * slots, dtype=jnp.int32)[:, None]
    line_slot = line // (2 * capacity) * capacity + line % capacity
    line_half = line // capacity % 2
    twice = jnp.concatenate((target, target), axis=0)
    factor = jnp.concatenate((jnp.ones_like(probs), factor), axis=0)
    side = (jnp.arange(2 * tok_rows, dtype=jnp.int32) // tok_rows)[None, :]
    spread = sum(
        jnp.where((line_slot == twice[None, :, k]) & (line_half == side), factor[None, :, k], 0.0)
        for k in range(top)
    ).astype(BF16)
    send = dot(spread, jnp.concatenate((tokens, out_grad), axis=0)).astype(BF16)

    def exchange(value, lines):
        return lax.all_to_all(
            value.reshape(experts, lines, -1), "expert", split_axis=0, concat_axis=0, tiled=True
        )

    send, core, target = lax.optimization_barrier((send, core, target))
    received, core, target = lax.optimization_barrier(
        (exchange(send, 2 * capacity), core, target)
    )
    d_gate, d_up, act, prob_part, rows_own, rows_other, scaled_own, scaled_other = hidden(
        received.reshape(experts, 2, capacity, width), weights, core
    )

    def add(*values):
        return sum(value.astype(F32) for value in values).astype(BF16)

    def swapped(value):
        return lax.ppermute(value, "dp", swap)

    def grad_of(left, right):
        return dot_rows(left, right).astype(BF16)

    other = []
    for lines, grad in ((scaled_other, act), (rows_other, d_gate), (rows_other, d_up)):
        if other:
            lines, grad, other[-1] = lax.optimization_barrier((lines, grad, other[-1]))
        other.append(grad_of(lines, grad))
    other = [swapped(part) for part in other]
    own_other = other
    own = [
        grad_of(lines, grad) for lines, grad in ((scaled_own, act), (rows_own, d_gate), (rows_own, d_up))
    ]
    pairs = jnp.zeros((chips * LANES, 3 * ff), BF16)
    for n, mine, theirs in zip((2, 0, 1), own, own_other, strict=True):
        pairs = lax.dynamic_update_slice(pairs, add(mine, theirs), (0, n * ff))
    weight_grad = lax.psum_scatter(
        pairs,
        "dp",
        scatter_dimension=0,
        axis_index_groups=[[2 * z + c for z in range(chips)] for c in range(2)],
        tiled=True,
    )[None]
    back = exchange(route_back(d_gate, d_up, weights, prob_part), capacity)

    back = back.reshape(slots, width + BLOCK)
    slot = jnp.arange(slots, dtype=jnp.int32)[:, None]
    match = [slot == target[None, :, k] for k in range(top)]
    placing = (match[0] | match[1]).astype(BF16)
    token_grad = dot_rows(placing, back[:, :width]).astype(BF16)
    prob_back = back[:, width].astype(F32)
    prob_grad = jnp.stack(
        [jnp.sum(jnp.where(m, prob_back[:, None], 0.0), axis=0) for m in match], axis=1
    )
    prob_grad = (prob_grad / probs).astype(BF16)
    return (token_grad, prob_grad, weight_grad)


def solution(mesh):
    in_specs = (
        P(("dp", "expert"), None),
        P(("dp", "expert"), None),
        P(("dp", "expert"), None),
        P(("dp", "expert"), None),
        P("dp"),
        P("expert", "dp", None),
        P("expert", "dp", None),
        P("expert", "dp", None),
    )
    out_specs = (P(("dp", "expert"), None), P(("dp", "expert"), None), P("expert", "dp", None))
    return jax.shard_map(
        per_device, mesh=mesh, in_specs=in_specs, out_specs=out_specs, check_vma=False
    )
```

```python
import jax
import jax.numpy as jnp
from jax import lax
from jax.experimental import pallas as pl
from jax.experimental.pallas import tpu as pltpu
from jax.sharding import PartitionSpec as P

F32 = jnp.float32
BF16 = jnp.bfloat16
VMEM_LIMIT = 56 * 1024 * 1024
LANES = 128
BLOCK = 256


def dot(left, right):
    return jnp.dot(left, right, preferred_element_type=F32)


def dot_rows(left, right):
    return lax.dot_general(left, right, (((0,), (0,)), ((), ())), preferred_element_type=F32)


def dot_last(left, right):
    return lax.dot_general(left, right, (((1,), (1,)), ((), ())), preferred_element_type=F32)


def params():
    return pltpu.CompilerParams(
        vmem_limit_bytes=VMEM_LIMIT, dimension_semantics=("arbitrary",)
    )


def hidden(received, weights, core):
    experts, _, capacity, width = received.shape
    slots, ff = experts * capacity, weights.shape[2]

    def body(s_ref, rows_ref, scaled_ref, w_ref, gate_ref, up_ref, act_ref, prob_ref, *apart):
        rows = rows_ref[...].reshape(slots, width)
        scaled = scaled_ref[...].reshape(slots, width)
        gate = dot(rows, w_ref[0])
        up = dot(rows, w_ref[1])
        back = dot(scaled, w_ref[2])
        sig = jax.nn.sigmoid(gate)
        silu = gate * sig
        act = (silu * up).astype(BF16)
        d_gate = (back * up * (sig + silu * (1.0 - sig))).astype(BF16)
        d_up = (back * silu).astype(BF16)
        for j in range(ff // BLOCK):

            @pl.when(pl.program_id(0) == j)
            def _():
                at = slice(j * BLOCK, (j + 1) * BLOCK)
                gate_ref[:, at] = d_gate
                up_ref[:, at] = d_up
                act_ref[:, at] = act

        part = jnp.sum(act.astype(F32) * back, axis=1, keepdims=True)

        @pl.when(pl.program_id(0) == 0)
        def _():
            prob_ref[...] = part
            first = s_ref[0] == 0
            for value, own_ref, other_ref in ((rows, *apart[:2]), (scaled, *apart[2:])):
                for n in range(width // (2 * LANES)):
                    at = slice(n * LANES, (n + 1) * LANES)
                    low = value[:, 2 * n * LANES : (2 * n + 1) * LANES]
                    high = value[:, (2 * n + 1) * LANES : (2 * n + 2) * LANES]
                    own_ref[:, at] = jnp.where(first, low, high)
                    other_ref[:, at] = jnp.where(first, high, low)

        @pl.when(pl.program_id(0) > 0)
        def _():
            prob_ref[...] += part

    return pl.pallas_call(
        body,
        grid_spec=pltpu.PrefetchScalarGridSpec(
            num_scalar_prefetch=1,
            grid=(ff // BLOCK,),
            in_specs=[
                pl.BlockSpec((experts, 1, capacity, width), lambda j, s: (0, 0, 0, 0)),
                pl.BlockSpec((experts, 1, capacity, width), lambda j, s: (0, 1, 0, 0)),
                pl.BlockSpec((3, width, BLOCK), lambda j, s: (0, 0, j)),
            ],
            out_specs=[pl.BlockSpec(memory_space=pltpu.VMEM)] * 3
            + [pl.BlockSpec((slots, 1), lambda j, s: (0, 0))]
            + [pl.BlockSpec(memory_space=pltpu.VMEM)] * 4,
        ),
        out_shape=[pltpu.VMEM((slots, ff), BF16)] * 3
        + [jax.ShapeDtypeStruct((slots, 1), F32)]
        + [pltpu.VMEM((slots, width // 2), BF16)] * 4,
        compiler_params=params(),
        name="hidden",
    )(core[None].astype(jnp.int32), received, received, weights)


def route_back(d_gate, d_up, weights, prob):
    slots, width, ff = d_gate.shape[0], *weights.shape[1:]
    steps = width // BLOCK

    def body(gate_ref, up_ref, w_ref, prob_ref, out_ref):
        @pl.when(pl.program_id(0) < steps)
        def _():
            value = dot_last(gate_ref[...], w_ref[0]) + dot_last(up_ref[...], w_ref[1])
            out_ref[...] = value.astype(BF16)

        @pl.when(pl.program_id(0) == steps)
        def _():
            out_ref[...] = jnp.broadcast_to(prob_ref[...], (slots, BLOCK)).astype(BF16)

    return pl.pallas_call(
        body,
        grid=(steps + 1,),
        in_specs=[
            pl.BlockSpec((slots, ff), lambda i: (0, 0)),
            pl.BlockSpec((slots, ff), lambda i: (0, 0)),
            pl.BlockSpec((2, BLOCK, ff), lambda i: (0, jnp.minimum(i, steps - 1), 0)),
            pl.BlockSpec((slots, 1), lambda i: (0, 0)),
        ],
        out_specs=pl.BlockSpec((slots, BLOCK), lambda i: (0, i)),
        out_shape=jax.ShapeDtypeStruct((slots, width + BLOCK), BF16),
        compiler_params=params(),
        name="route_back",
    )(d_gate, d_up, weights, prob)


def per_device(
    tokens, out_grad, routes, route_probs, kept_count, gate_weight, up_weight, down_weight
):
    tok_rows, width = tokens.shape
    top = routes.shape[1]
    experts = lax.axis_size("expert")
    chips = lax.axis_size("dp") // 2
    capacity = 2 * tok_rows * top // experts
    slots = experts * capacity
    ff = gate_weight.shape[2]
    dp = lax.axis_index("dp")
    core = dp % 2
    swap = [(2 * z + c, 2 * z + 1 - c) for z in range(chips) for c in range(2)]

    weights = lax.all_gather(
        jnp.concatenate((gate_weight, up_weight, down_weight), axis=0), "dp", axis=1, tiled=True
    )

    row = lax.axis_index("expert") * tok_rows + jnp.arange(tok_rows, dtype=jnp.int32)
    kept = row < kept_count[0]
    flat = routes.reshape(-1)
    onehot = (flat[:, None] == jnp.arange(experts, dtype=jnp.int32)[None, :]).astype(jnp.int32)
    before = jnp.cumsum(onehot, axis=0) - onehot
    position = jnp.sum(before * onehot, axis=1)
    target = (flat * capacity + position).reshape(tok_rows, top)
    probs = route_probs.astype(F32)
    factor = jnp.where(kept[:, None], probs, 0.0)
    line = jnp.arange(2 * slots, dtype=jnp.int32)[:, None]
    line_slot = line // (2 * capacity) * capacity + line % capacity
    line_half = line // capacity % 2
    twice = jnp.concatenate((target, target), axis=0)
    factor = jnp.concatenate((jnp.ones_like(probs), factor), axis=0)
    side = (jnp.arange(2 * tok_rows, dtype=jnp.int32) // tok_rows)[None, :]
    spread = sum(
        jnp.where((line_slot == twice[None, :, k]) & (line_half == side), factor[None, :, k], 0.0)
        for k in range(top)
    ).astype(BF16)
    send = dot(spread, jnp.concatenate((tokens, out_grad), axis=0)).astype(BF16)

    def exchange(value, lines):
        return lax.all_to_all(
            value.reshape(experts, lines, -1), "expert", split_axis=0, concat_axis=0, tiled=True
        )

    send, core, target = lax.optimization_barrier((send, core, target))
    received, core, target = lax.optimization_barrier(
        (exchange(send, 2 * capacity), core, target)
    )
    d_gate, d_up, act, prob_part, rows_own, rows_other, scaled_own, scaled_other = hidden(
        received.reshape(experts, 2, capacity, width), weights, core
    )

    def add(*values):
        return sum(value.astype(F32) for value in values).astype(BF16)

    def swapped(value):
        return lax.ppermute(value, "dp", swap)

    def grad_of(left, right):
        return dot_rows(left, right).astype(BF16)

    other = []
    for lines, grad in ((scaled_other, act), (rows_other, d_gate), (rows_other, d_up)):
        if other:
            lines, grad, other[-1] = lax.optimization_barrier((lines, grad, other[-1]))
        other.append(grad_of(lines, grad))
    other = [swapped(part) for part in other]
    own_other = other
    own = [
        grad_of(lines, grad) for lines, grad in ((scaled_own, act), (rows_own, d_gate), (rows_own, d_up))
    ]
    own = lax.optimization_barrier(own)
    pairs = jnp.zeros((chips * LANES, 3 * ff), BF16)
    for n, mine, theirs in zip((2, 0, 1), own, own_other, strict=True):
        pairs = lax.dynamic_update_slice(pairs, add(mine, theirs), (0, n * ff))
    weight_grad = lax.psum_scatter(
        pairs,
        "dp",
        scatter_dimension=0,
        axis_index_groups=[[2 * z + c for z in range(chips)] for c in range(2)],
        tiled=True,
    )[None]
    back = exchange(route_back(d_gate, d_up, weights, prob_part), capacity)

    back = back.reshape(slots, width + BLOCK)
    slot = jnp.arange(slots, dtype=jnp.int32)[:, None]
    match = [slot == target[None, :, k] for k in range(top)]
    placing = (match[0] | match[1]).astype(BF16)
    token_grad = dot_rows(placing, back[:, :width]).astype(BF16)
    prob_back = back[:, width].astype(F32)
    prob_grad = jnp.stack(
        [jnp.sum(jnp.where(m, prob_back[:, None], 0.0), axis=0) for m in match], axis=1
    )
    prob_grad = (prob_grad / probs).astype(BF16)
    return (token_grad, prob_grad, weight_grad)


def solution(mesh):
    in_specs = (
        P(("dp", "expert"), None),
        P(("dp", "expert"), None),
        P(("dp", "expert"), None),
        P(("dp", "expert"), None),
        P("dp"),
        P("expert", "dp", None),
        P("expert", "dp", None),
        P("expert", "dp", None),
    )
    out_specs = (P(("dp", "expert"), None), P(("dp", "expert"), None), P("expert", "dp", None))
    return jax.shard_map(
        per_device, mesh=mesh, in_specs=in_specs, out_specs=out_specs, check_vma=False
    )
```
